256 devices in a mesh: hid: 32 (over y, z), wid: 4 (over x), ad: 2 (over core).
Axes of the slice: x: 4, y: 4, z: 8, core: 2. Of those that a mesh axis runs over, the one named last changes fastest.
Arguments:
- activations: bfloat16 [1536, 2, 8192], P(None, None, ('wid', 'ad')), may hold values from -6 to 6
- row_adapter_index: int32 [1536, 2], replicated, may hold values from 0 to 127, as said below
- gate_up_weight: bfloat16 [8192, 2, 14848], P(('wid', 'ad'), None, 'hid'), may hold values from -0.0625 to 0.0625
- down_weight: bfloat16 [14848, 8192], P('hid', ('wid', 'ad')), may hold values from -0.046875 to 0.046875
- adapter_shrink_weight: bfloat16 [128, 2, 64, 8192], P(('hid', 'wid'), 'ad'), may hold values from -0.0625 to 0.0625
- adapter_expand_weight: bfloat16 [128, 2, 64, 14848], P(('hid', 'wid'), 'ad'), may hold values from -0.75 to 0.75
Outputs:
- layer_out: bfloat16 [1536, 2, 8192], P('hid', None, ('wid', 'ad'))
The draws below stay inside these ranges and needn't reach their ends.
Inputs may be any that keep to these rules, and one draw needn't show every extreme that they name: `row_adapter_index`: call rows 48 * h to 48 * h + 47 of both batches together block h. In every block no adapter is named more than 2 times, and one and the same adapter is named exactly 2 times in every block.
All inputs are finite; a program needn't handle non-finite values.
Results may differ from the reference program's by a relative error of at most 0.0064.
Values may be sent and summed in bfloat16 or wider, within the bound.
No kernel may reach another device: no remote copies, remote signals or barrier semaphores. Data moves between devices by JAX's collectives and lax.ppermute only.
A program may use at most 128 MiB of HBM per device.

```python
import jax
import jax.numpy as jnp
from jax import lax

MODEL_DIM = 8192
HIDDEN_UNITS = 14848
ADAPTER_RANK = 64
NB = 2
ROWS_BLK = 48
ROWS = 1536
ADAPTER_TOTAL = 128
CAP = 2
N_HID = 32


def draw_row_adapter_index(key, part):
    blocks = ROWS // ROWS_BLK
    per_block = ROWS_BLK * NB
    tickets = ADAPTER_TOTAL * CAP
    key_hot, key_bias, key_score, key_place = jax.random.split(key, 4)
    hot_adapter = jax.random.randint(key_hot, (), 0, ADAPTER_TOTAL)
    adapter_bias = jax.random.randint(key_bias, (ADAPTER_TOTAL,), 0, 4) * 16384
    ticket_adapter = jnp.arange(tickets, dtype=jnp.int32) % ADAPTER_TOTAL
    scores = jax.random.randint(key_score, (blocks, tickets), 0, 65536)
    scores = scores + adapter_bias[ticket_adapter][None, :]
    scores = scores + jnp.where(ticket_adapter == hot_adapter, 1048576, 0)[None, :]
    scores = scores * 1024 + jnp.arange(tickets, dtype=jnp.int32)[None, :]
    _, chosen = lax.top_k(scores, per_block)
    picked = ticket_adapter[chosen]
    shuffle = jax.vmap(lambda block_key: jax.random.permutation(block_key, per_block))(jax.random.split(key_place, blocks))
    placed = jnp.take_along_axis(picked, shuffle, axis=1)
    return placed.reshape(ROWS, NB).astype(jnp.int32)


def block_scale(stream_key, shape, cuts, low, top_value):
    def one(axis_at, parts):
        steps = jax.random.uniform(jax.random.fold_in(jax.random.fold_in(stream_key, 6), axis_at), (parts,), jnp.float32, low / len(cuts), top_value / len(cuts))
        return jnp.repeat(jnp.exp(steps), shape[axis_at] // parts).reshape((-1,) + (1,) * (len(shape) - axis_at - 1))

    gain = one(*cuts[0])
    for cut in cuts[1:]:
        gain = gain * one(*cut)
    return gain


def scatter_about(rng, extent, scale, reach, cuts=(), held_as=jnp.bfloat16):
    drawn = scale * jax.random.normal(rng, extent, jnp.float32)
    if cuts:
        drawn = drawn * block_scale(rng, extent, cuts, -0.22, 0.18)
    return jnp.clip(drawn, -reach, reach).astype(held_as)


def setup_inputs(seed: int = 0) -> dict:
    splits = jax.random.split(jax.random.key(seed), 7)
    return {
        "activations": scatter_about(splits[0], (ROWS, NB, MODEL_DIM), 1.0, 6.0, ((2, 8),)),
        "row_adapter_index": draw_row_adapter_index(jax.random.fold_in(splits[6], 71), 0),
        "gate_up_weight": scatter_about(splits[2], (MODEL_DIM, 2, HIDDEN_UNITS), MODEL_DIM ** -0.5, 0.0625, ((0, 8), (2, 32))),
        "down_weight": scatter_about(splits[3], (HIDDEN_UNITS, MODEL_DIM), HIDDEN_UNITS ** -0.5, 0.046875, ((0, 32), (1, 8))),
        "adapter_shrink_weight": scatter_about(splits[4], (ADAPTER_TOTAL, 2, ADAPTER_RANK, MODEL_DIM), MODEL_DIM ** -0.5, 0.0625, ((0, 128), (1, 2))),
        "adapter_expand_weight": scatter_about(splits[5], (ADAPTER_TOTAL, 2, ADAPTER_RANK, HIDDEN_UNITS), ADAPTER_RANK ** -0.5, 0.75, ((0, 128), (1, 2))),
    }


def reference(activations, row_adapter_index, gate_up_weight, down_weight, adapter_shrink_weight, adapter_expand_weight):
    total_rows, batch_count, model_width = activations.shape
    flat_acts = activations.reshape(-1, model_width)
    flat_ids = row_adapter_index.reshape(-1).astype(jnp.int32)
    row_total = flat_acts.shape[0]
    base_proj = jnp.dot(flat_acts, gate_up_weight.reshape(model_width, -1), preferred_element_type=jnp.float32)
    base_proj = base_proj.reshape(row_total, 2, HIDDEN_UNITS)
    sorted_rows = jnp.argsort(flat_ids, stable=True).astype(jnp.int32)
    counts = jnp.sum((flat_ids[None, :] == jnp.arange(ADAPTER_TOTAL, dtype=jnp.int32)[:, None]).astype(jnp.int32), axis=1).astype(jnp.int32)
    offsets = (jnp.cumsum(counts) - counts).astype(jnp.int32)
    most_rows = CAP * N_HID

    def per_adapter(accumulated, adapter_number):
        slot_index = offsets[adapter_number] + jnp.arange(most_rows, dtype=jnp.int32)
        is_valid = jnp.arange(most_rows, dtype=jnp.int32) < counts[adapter_number]
        rows_idx = jnp.where(is_valid, sorted_rows[jnp.minimum(slot_index, row_total - 1)], row_total).astype(jnp.int32)
        picked = flat_acts[jnp.minimum(rows_idx, row_total - 1)]
        shrink_weight = adapter_shrink_weight[adapter_number]
        rank_values = jnp.einsum("nd,prd->pnr", picked.astype(jnp.float32), shrink_weight.astype(jnp.float32)).astype(jnp.bfloat16)
        row_updates = jnp.einsum("iah,ihj->aij", rank_values.astype(jnp.float32), adapter_expand_weight[adapter_number].astype(jnp.float32)).astype(jnp.bfloat16)
        accumulated = accumulated.at[rows_idx].add(row_updates.astype(jnp.float32), mode="drop")
        return accumulated, None

    deltas, _ = lax.scan(per_adapter, jnp.zeros((row_total, 2, HIDDEN_UNITS), jnp.float32), jnp.arange(ADAPTER_TOTAL, dtype=jnp.int32))
    gate_values = base_proj[:, 0] + deltas[:, 0]
    up_values = base_proj[:, 1] + deltas[:, 1]
    hidden = (jax.nn.silu(gate_values) * up_values).astype(jnp.bfloat16)
    result = jnp.dot(hidden, down_weight, preferred_element_type=jnp.float32).astype(jnp.bfloat16)
    return result.reshape(total_rows, batch_count, model_width)
```

```python
import jax
import jax.numpy as jnp
from jax import lax
from jax.sharding import Mesh, PartitionSpec as P

CHUNKS = 3
Y, Z = 4, 8
F32 = jnp.float32
BF16 = jnp.bfloat16


def local(activations, row_adapter_index, gate_up_weight, down_weight, shrink, expand):
    hid = lax.axis_index(("y", "z"))
    wid = lax.axis_index("wid")
    ad = lax.axis_index("ad")
    n_hid = Y * Z
    total_rows, batches, width = activations.shape
    rows = total_rows * batches
    block = rows // n_hid
    part = block // CHUNKS
    units = down_weight.shape[0]
    rank = shrink.shape[2]
    slots = 2 * n_hid

    by_owner = expand[0, 0].reshape(rank, n_hid, units).transpose(1, 0, 2)
    expand_all = lax.all_to_all(by_owner, ("y", "z"), split_axis=0, concat_axis=0, tiled=True)

    def to_chunks(flat):
        return flat.reshape((n_hid, CHUNKS, part) + flat.shape[1:]).swapaxes(0, 1)

    acts = activations.reshape(n_hid, CHUNKS, part // 2, 2, width)
    acts = acts.swapaxes(0, 1).reshape(rows, width)
    ids = row_adapter_index.reshape(n_hid, block)
    same = ids[:, :, None] == ids[:, None, :]
    earlier = jnp.arange(block)[None, :] < jnp.arange(block)[:, None]
    place = jnp.sum((same & earlier[None]).astype(jnp.int32), axis=2)
    slot = 2 * jnp.arange(n_hid, dtype=jnp.int32)[:, None] + place
    owner, cls = ids // 4, ids % 4
    send_code = jnp.where(owner == hid, cls * slots + slot, -1)
    recv_code = jnp.where(cls == wid, owner * slots + slot, -1)
    send_code = to_chunks(send_code.reshape(rows)).reshape(rows)
    recv_code = to_chunks(recv_code.reshape(rows)).reshape(CHUNKS, rows // CHUNKS)

    pick = (jnp.arange(4 * slots, dtype=jnp.int32)[:, None] == send_code[None, :]).astype(BF16)
    picked = jnp.dot(pick, acts, preferred_element_type=F32).astype(BF16)
    picked = picked.reshape(4, 1, slots, width)
    picked = jnp.broadcast_to(picked, (4, 2, slots, width)).reshape(8, slots, width)
    got = lax.all_to_all(picked, ("wid", "ad"), split_axis=0, concat_axis=0, tiled=True)
    inner = jnp.einsum(
        "xsf,jxf->sj", got, shrink[0, 0].reshape(rank, 8, width), preferred_element_type=F32
    ).astype(BF16)
    inner_all = lax.all_to_all(
        jnp.broadcast_to(inner[None], (n_hid, slots, rank)),
        ("y", "z"), split_axis=0, concat_axis=0, tiled=True,
    )
    terms = jnp.einsum(
        "hsj,hju->hsu", inner_all, expand_all, preferred_element_type=F32
    ).astype(BF16).reshape(n_hid * slots, units)

    weights = gate_up_weight.transpose(1, 0, 2)
    chunk_rows = rows // CHUNKS
    half = chunk_rows // 2
    quarter = half // 4
    is_mine = (jnp.arange(2) == ad)[:, None, None]
    swap = [(0, 1), (1, 0)]
    acts = acts.reshape(CHUNKS, chunk_rows, width)
    outs = []
    for c in range(CHUNKS):
        base = jnp.einsum("rd,pdu->pru", acts[c], weights, preferred_element_type=F32)
        place_rows = (recv_code[c][:, None] == jnp.arange(n_hid * slots, dtype=jnp.int32)[None, :]).astype(BF16)
        delta = jnp.dot(place_rows, terms, preferred_element_type=F32).astype(BF16)
        value = base + jnp.where(is_mine, delta.astype(F32)[None], 0.0)
        away = lax.dynamic_slice_in_dim(value, (1 - ad) * half, half, 1).astype(BF16)
        keep = lax.dynamic_slice_in_dim(value, ad * half, half, 1)
        pair = keep + lax.ppermute(away, "ad", swap).astype(F32)
        pair = pair.astype(BF16).reshape(2, 4, quarter, units).swapaxes(0, 1)
        parts = lax.all_to_all(pair, "wid", split_axis=0, concat_axis=0, tiled=True)
        summed = jnp.sum(parts.astype(F32), axis=0)
        hidden = (jax.nn.silu(summed[0]) * summed[1]).astype(BF16)
        hidden = lax.all_gather(hidden, ("ad", "wid"), axis=0, tiled=True)
        partial = jnp.dot(hidden, down_weight, preferred_element_type=F32).astype(BF16)
        partial = lax.psum_scatter(partial, "y", scatter_dimension=0, tiled=True)
        outs.append(lax.psum_scatter(partial, "z", scatter_dimension=0, tiled=True))
    out = jnp.concatenate(outs, axis=0)
    return out.reshape(total_rows // n_hid, batches, -1)


def solution(mesh):
    grid = Mesh(mesh.devices.reshape(Y, Z, 4, 2), ("y", "z", "wid", "ad"))
    hid = ("y", "z")
    in_specs = (
        P(None, None, ("wid", "ad")),
        P(),
        P(("wid", "ad"), None, hid),
        P(hid, ("wid", "ad")),
        P(("y", "z", "wid"), "ad", None, None),
        P(("y", "z", "wid"), "ad", None, None),
    )
    return jax.shard_map(local, mesh=grid, in_specs=in_specs, out_specs=P(hid, None, ("wid", "ad")), check_vma=False)
```

```python
import jax
import jax.numpy as jnp
from jax import lax
from jax.sharding import Mesh, PartitionSpec as P

CHUNKS = 3
Y, Z, W = 4, 8, 4
F32 = jnp.float32
BF16 = jnp.bfloat16


def order(n):
    return sorted(range(1, n), key=lambda k: -min(k, n - k))


def shift(value, axis, n, k):
    return lax.ppermute(value, axis, [(i, (i + k) % n) for i in range(n)])


def swap(value):
    return lax.ppermute(value, "ad", [(0, 1), (1, 0)])


def exchange(blocks, axis, n, dim=0):
    me = lax.axis_index(axis)
    own = lax.dynamic_index_in_dim(blocks, me, dim, keepdims=False)
    got = []
    for k in order(n):
        away = lax.dynamic_index_in_dim(blocks, (me + k) % n, dim, keepdims=False)
        got.append((k, shift(away.astype(BF16), axis, n, k)))
    return own, got


def collect(own, got, axis, n):
    me = lax.axis_index(axis)
    full = jnp.zeros((n,) + own.shape, own.dtype)
    full = lax.dynamic_update_index_in_dim(full, own, me, 0)
    for k, value in got:
        full = lax.dynamic_update_index_in_dim(full, value, (me + n - k) % n, 0)
    return full


def reduce_blocks(blocks, axis, n, dim=0):
    own, got = exchange(blocks, axis, n, dim)
    total = own.astype(F32)
    for _, value in got:
        total = total + value.astype(F32)
    return total


def gather_blocks(own, axis, n):
    return collect(own, [(k, shift(own, axis, n, k)) for k in order(n)], axis, n)


def local(activations, row_adapter_index, gate_up_weight, down_weight, shrink, expand):
    hid = lax.axis_index(("y", "z"))
    wid = lax.axis_index("wid")
    ad = lax.axis_index("ad")
    n_hid = Y * Z
    total_rows, batches, width = activations.shape
    rows = total_rows * batches
    block = rows // n_hid
    part = block // CHUNKS
    units = down_weight.shape[0]
    rank = shrink.shape[2]
    slots = 2 * n_hid

    by_owner = expand[0, 0].reshape(rank, n_hid, units).transpose(1, 0, 2)
    by_owner, activations = lax.optimization_barrier((by_owner, activations))
    with jax.named_scope("expand_send"):
        expand_all = lax.all_to_all(by_owner, ("y", "z"), split_axis=0, concat_axis=0, tiled=True)

    def to_chunks(flat):
        return flat.reshape((n_hid, CHUNKS, part) + flat.shape[1:]).swapaxes(0, 1)

    acts = activations.reshape(n_hid, CHUNKS, part // 2, 2, width)
    acts = acts.swapaxes(0, 1).reshape(rows, width)
    acts = lax.optimization_barrier(acts)
    ids = row_adapter_index.reshape(n_hid, block)
    same = ids[:, :, None] == ids[:, None, :]
    earlier = jnp.arange(block)[None, :] < jnp.arange(block)[:, None]
    place = jnp.sum((same & earlier[None]).astype(jnp.int32), axis=2)
    slot = 2 * jnp.arange(n_hid, dtype=jnp.int32)[:, None] + place
    owner, cls = ids // W, ids % W
    send_code = jnp.where(owner == hid, cls * slots + slot, -1)
    recv_code = jnp.where(cls == wid, owner * slots + slot, -1)
    send_code = to_chunks(send_code.reshape(rows)).reshape(rows)
    recv_code = to_chunks(recv_code.reshape(rows)).reshape(CHUNKS, rows // CHUNKS)

    with jax.named_scope("pick"):
        pick = (jnp.arange(W * slots, dtype=jnp.int32)[:, None] == send_code[None, :]).astype(BF16)
        picked = jnp.dot(pick, acts, preferred_element_type=F32).astype(BF16)
    picked = picked.reshape(W, slots, width)
    with jax.named_scope("rows_x"):
        mine = collect(*exchange(picked, "wid", W), "wid", W)
    with jax.named_scope("rows_ad"):
        theirs = swap(mine)
    first = jnp.where(ad == 0, mine, theirs)
    second = jnp.where(ad == 0, theirs, mine)
    shrink_blocks = shrink[0, 0].reshape(rank, W, 2, width)
    inner = jnp.einsum("xsf,jxf->sj", first, shrink_blocks[:, :, 0], preferred_element_type=F32)
    inner = inner + jnp.einsum("xsf,jxf->sj", second, shrink_blocks[:, :, 1], preferred_element_type=F32)
    inner = jnp.broadcast_to(inner.astype(BF16)[None], (n_hid, slots, rank))
    inner, expand_all = lax.optimization_barrier((inner, expand_all))
    with jax.named_scope("inner_send"):
        inner_all = lax.all_to_all(inner, ("y", "z"), split_axis=0, concat_axis=0, tiled=True)
    with jax.named_scope("terms"):
        terms = jnp.einsum(
            "hsj,hju->hsu", inner_all, expand_all, preferred_element_type=F32
        ).astype(BF16).reshape(n_hid * slots, units)

    weights = gate_up_weight.transpose(1, 0, 2)
    chunk_rows = rows // CHUNKS
    half = chunk_rows // 2
    quarter = half // W
    is_mine = (jnp.arange(2) == ad)[:, None, None]
    acts = acts.reshape(CHUNKS, chunk_rows, width)
    outs = []
    for c in range(CHUNKS):
        base = jnp.einsum("rd,pdu->pru", acts[c], weights, preferred_element_type=F32)
        place_rows = (recv_code[c][:, None] == jnp.arange(n_hid * slots, dtype=jnp.int32)[None, :]).astype(BF16)
        delta = jnp.dot(place_rows, terms, preferred_element_type=F32).astype(BF16)
        value = base + jnp.where(is_mine, delta.astype(F32)[None], 0.0)
        away = lax.dynamic_slice_in_dim(value, (1 - ad) * half, half, 1).astype(BF16)
        keep = lax.dynamic_slice_in_dim(value, ad * half, half, 1)
        pair = keep + swap(away).astype(F32)
        summed = reduce_blocks(pair.astype(BF16).reshape(2, W, quarter, units), "wid", W, 1)
        hidden = (jax.nn.silu(summed[0]) * summed[1]).astype(BF16)
        hidden = gather_blocks(hidden, "wid", W).reshape(half, units)
        other = swap(hidden)
        full = jnp.concatenate(
            [jnp.where(ad == 0, hidden, other), jnp.where(ad == 0, other, hidden)], axis=0
        )
        partial = jnp.dot(full, down_weight, preferred_element_type=F32).astype(BF16)
        partial = reduce_blocks(partial.reshape(Y, chunk_rows // Y, -1), "y", Y)
        partial = reduce_blocks(partial.astype(BF16).reshape(Z, chunk_rows // n_hid, -1), "z", Z)
        outs.append(partial.astype(BF16))
    out = jnp.concatenate(outs, axis=0)
    return out.reshape(total_rows // n_hid, batches, -1)


def solution(mesh):
    grid = Mesh(mesh.devices.reshape(Y, Z, W, 2), ("y", "z", "wid", "ad"))
    hid = ("y", "z")
    in_specs = (
        P(None, None, ("wid", "ad")),
        P(),
        P(("wid", "ad"), None, hid),
        P(hid, ("wid", "ad")),
        P(("y", "z", "wid"), "ad", None, None),
        P(("y", "z", "wid"), "ad", None, None),
    )
    return jax.shard_map(local, mesh=grid, in_specs=in_specs, out_specs=P(hid, None, ("wid", "ad")), check_vma=False)
```

```python
import jax
import jax.numpy as jnp
from jax import lax
from jax.sharding import Mesh, PartitionSpec as P

CHUNKS = 2
Y, Z, W = 4, 8, 4
F32 = jnp.float32
BF16 = jnp.bfloat16


def swap(value):
    return lax.ppermute(value, "ad", [(0, 1), (1, 0)])


def by_core(ad, mine, theirs):
    return jnp.where(ad == 0, mine, theirs), jnp.where(ad == 0, theirs, mine)


def send(blocks, axis):
    return lax.all_to_all(blocks, axis, split_axis=0, concat_axis=0, tiled=True)


def spread(value, axis, n):
    return send(jnp.broadcast_to(value[None], (n,) + value.shape), axis)


def halve(blocks, axis, flip):
    me = lax.axis_index(axis)
    across, beside = [(i, 3 - i) for i in range(4)], [(i, i ^ 1) for i in range(4)]
    if flip:
        groups, in_first, second = ((0, 1), (2, 3)), me < 2, me % 2 == 1
        steps = (across, beside)
    else:
        groups, in_first, second = ((0, 3), (1, 2)), (me == 0) | (me == 3), me >= 2
        steps = (beside, across)
    one, two = (jnp.stack([blocks[b] for b in group]) for group in groups)
    away = jnp.where(in_first, two, one).astype(BF16)
    held = jnp.where(in_first, one, two) + lax.ppermute(away, axis, steps[0]).astype(F32)
    away = jnp.where(second, held[0], held[1]).astype(BF16)
    return jnp.where(second, held[1], held[0]) + lax.ppermute(away, axis, steps[1]).astype(F32)


def local(activations, row_adapter_index, gate_up_weight, down_weight, shrink, expand):
    hid = lax.axis_index(("y", "z"))
    wid = lax.axis_index("wid")
    ad = lax.axis_index("ad")
    n_hid = Y * Z
    total_rows, batches, width = activations.shape
    rows = total_rows * batches
    block = rows // n_hid
    part = block // CHUNKS
    units = down_weight.shape[0]
    rank = shrink.shape[2]
    slots = 2 * n_hid

    by_owner = expand[0, 0].reshape(rank, n_hid, units).transpose(1, 0, 2)
    by_owner, activations = lax.optimization_barrier((by_owner, activations))
    with jax.named_scope("expand_send"):
        expand_all = send(by_owner, ("y", "z"))

    def to_chunks(flat):
        flat = flat.reshape((Y, Z, CHUNKS, -1) + flat.shape[1:])
        return flat.transpose((2, 1, 0) + tuple(range(3, flat.ndim)))

    acts = to_chunks(activations).reshape(rows, width)
    acts = lax.optimization_barrier(acts)
    ids = row_adapter_index.reshape(n_hid, block)
    same = ids[:, :, None] == ids[:, None, :]
    earlier = jnp.arange(block)[None, :] < jnp.arange(block)[:, None]
    place = jnp.sum((same & earlier[None]).astype(jnp.int32), axis=2)
    slot = 2 * jnp.arange(n_hid, dtype=jnp.int32)[:, None] + place
    owner, cls = ids // W, ids % W
    send_code = jnp.where(owner == hid, cls * slots + slot, -1)
    recv_code = jnp.where(cls == wid, owner * slots + slot, -1)
    send_code = to_chunks(send_code.reshape(rows)).reshape(rows)
    recv_code = to_chunks(recv_code.reshape(rows)).reshape(CHUNKS, rows // CHUNKS)

    with jax.named_scope("pick"):
        pick = (jnp.arange(W * slots, dtype=jnp.int32)[:, None] == send_code[None, :]).astype(BF16)
        picked = jnp.dot(pick, acts, preferred_element_type=F32).astype(BF16)
    with jax.named_scope("rows_x"):
        mine = rows_x(picked.reshape(W, slots, width))
    with jax.named_scope("rows_ad"):
        theirs = swap(mine)
    first, second = by_core(ad, mine, theirs)
    shrink_blocks = shrink[0, 0].reshape(rank, W, 2, width)
    inner = jnp.einsum("xsf,jxf->sj", first, shrink_blocks[:, :, 0], preferred_element_type=F32)
    inner = inner + jnp.einsum("xsf,jxf->sj", second, shrink_blocks[:, :, 1], preferred_element_type=F32)
    inner, expand_all = lax.optimization_barrier((inner.astype(BF16), expand_all))
    with jax.named_scope("inner_send"):
        inner_all = spread(inner, ("y", "z"), n_hid)
    with jax.named_scope("terms"):
        terms = jnp.einsum(
            "hsj,hju->hsu", inner_all, expand_all, preferred_element_type=F32
        ).astype(BF16).reshape(n_hid * slots, units)

    weights = gate_up_weight.transpose(1, 2, 0)
    chunk_rows = rows // CHUNKS
    half = chunk_rows // 2
    piece = half // W
    is_mine = (jnp.arange(2) == ad)[:, None, None]
    acts = acts.reshape(CHUNKS, chunk_rows, width)
    outs = []
    for c in range(CHUNKS):
        base = jnp.einsum("pud,rd->pur", weights, acts[c], preferred_element_type=F32)
        place_rows = (recv_code[c][:, None] == jnp.arange(n_hid * slots, dtype=jnp.int32)[None, :]).astype(BF16)
        delta = jnp.einsum("su,rs->ur", terms, place_rows, preferred_element_type=F32).astype(BF16)
        value = base + jnp.where(is_mine, delta.astype(F32)[None], 0.0)
        value = value.reshape(2, units, 2, W, piece)
        away, keep = by_core(ad, value[:, :, 1], value[:, :, 0])
        pair = keep + swap(away.astype(BF16)).astype(F32)
        with jax.named_scope("gate_send"):
            gate = halve([pair[0, :, b] for b in range(W)], "wid", False)
            up = halve([pair[1, :, b] for b in range(W)], "wid", True)
        hidden = (jax.nn.silu(gate) * up).astype(BF16)
        with jax.named_scope("hidden_send"):
            hidden = spread(hidden, "wid", W)
        full = jnp.stack(by_core(ad, hidden, swap(hidden)))
        partial = jnp.einsum("awuq,ud->awqd", full, down_weight, preferred_element_type=F32)
        partial = partial.reshape(Z, Y, part, 2, -1)
        with jax.named_scope("y_send"):
            partial = jnp.concatenate(
                [halve([partial[:, b, :, f] for b in range(Y)], "y", f == 1) for f in range(2)], axis=-1
            ).astype(BF16)
        with jax.named_scope("z_send"):
            partial = jnp.sum(send(partial, "z").astype(F32), axis=0).astype(BF16)
        outs.append(partial)
    out = jnp.concatenate(outs, axis=0)
    return out.reshape(total_rows // n_hid, batches, -1)


def rows_x(blocks):
    me = lax.axis_index("wid")
    full = lax.dynamic_update_index_in_dim(
        jnp.zeros_like(blocks), lax.dynamic_index_in_dim(blocks, me, 0, keepdims=False), me, 0
    )
    for k in (2, 1, 3):
        away = lax.dynamic_index_in_dim(blocks, (me + k) % W, 0, keepdims=False)
        value = lax.ppermute(away, "wid", [(i, (i + k) % W) for i in range(W)])
        full = lax.dynamic_update_index_in_dim(full, value, (me + W - k) % W, 0)
    return full


def solution(mesh):
    grid = Mesh(mesh.devices.reshape(Y, Z, W, 2), ("y", "z", "wid", "ad"))
    hid = ("y", "z")
    in_specs = (
        P(None, None, ("wid", "ad")),
        P(),
        P(("wid", "ad"), None, hid),
        P(hid, ("wid", "ad")),
        P(("y", "z", "wid"), "ad", None, None),
        P(("y", "z", "wid"), "ad", None, None),
    )
    return jax.shard_map(local, mesh=grid, in_specs=in_specs, out_specs=P(hid, None, ("wid", "ad")), check_vma=False)
```

```python
import functools

import jax
import jax.numpy as jnp
from jax import lax
from jax.experimental import pallas as pl
from jax.experimental.pallas import tpu as pltpu
from jax.sharding import Mesh, PartitionSpec as P

CHUNKS = 2
Y, Z, W = 4, 8, 4
F32 = jnp.float32
BF16 = jnp.bfloat16
PAIRS = [(i, i ^ 1) for i in range(4)]
ACROSS = [(i, 3 - i) for i in range(4)]


def swap(value):
    return lax.ppermute(value, "ad", [(0, 1), (1, 0)])


def by_core(ad, mine, theirs):
    return jnp.where(ad == 0, mine, theirs), jnp.where(ad == 0, theirs, mine)


def send(blocks, axis):
    return lax.all_to_all(blocks, axis, split_axis=0, concat_axis=0, tiled=True)


def spread(value, axis, n):
    return send(jnp.broadcast_to(value[None], (n,) + value.shape), axis)


def ring_orders(me):
    side, far = me ^ 1, 3 - me
    return jnp.stack([me, far, side, 3 - side]), jnp.stack([me, side, far, far ^ 1])


def split_owners(expand, n, units):
    def body(x, o):
        for h in range(n):
            o[h] = x[:, h * units:(h + 1) * units]

    rank = expand.shape[0]
    return pl.pallas_call(
        body,
        out_shape=jax.ShapeDtypeStruct((n, rank, units), expand.dtype),
        cost_estimate=pl.CostEstimate(flops=0, bytes_accessed=4 * expand.size, transcendentals=0),
        name="split_owners",
    )(expand)


def order_rows(activations):
    total, batches, width = activations.shape
    count = total // (Y * Z * CHUNKS)
    rows = Y * count * batches

    def body(x, o):
        o[...] = x[...].reshape(rows, width)

    return pl.pallas_call(
        body,
        grid=(CHUNKS, Z),
        in_specs=[pl.BlockSpec((Y, None, count, batches, width), lambda c, z: (0, z, c, 0, 0))],
        out_specs=pl.BlockSpec((rows, width), lambda c, z: (c * Z + z, 0)),
        out_shape=jax.ShapeDtypeStruct((total * batches, width), activations.dtype),
        cost_estimate=pl.CostEstimate(flops=0, bytes_accessed=4 * activations.size, transcendentals=0),
        name="order_rows",
    )(activations.reshape(Y, Z, CHUNKS * count, batches, width))


def gate_up(orders, ad, acts, codes, weights, terms, chunk):
    _, units, width = weights.shape
    piece = acts.shape[0] // (CHUNKS * 2 * W)
    count = terms.shape[0]

    def one(x, code, w, t, core, p):
        value = lax.dot_general(x, w[p], (((1,), (1,)), ((), ())), preferred_element_type=F32)
        return value + jnp.where(core == p, t, 0.0)

    def body(s, xa, xk, ca, ck, w, t, ag, au, kg, ku):
        core = s[0]
        wide = lax.broadcasted_iota(jnp.int32, (piece, count), 1)
        for x, c, outs in ((xa, ca, (ag, au)), (xk, ck, (kg, ku))):
            place = (c[...] == wide).astype(BF16)
            term = jnp.dot(place, t[...], preferred_element_type=F32).astype(BF16).astype(F32)
            for p, o in enumerate(outs):
                o[...] = one(x[...], None, w, term, core, p).astype(o.dtype)

    def rows_of(away):
        def index(i, s):
            core = 1 - s[0] if away else s[0]
            return (chunk * 2 * W + core * W + s[1 + i], 0)
        return index

    def place_at(p):
        def index(i, s):
            return (s[5 + 4 * p + i], 0, 0)
        return index

    scalars = jnp.concatenate([ad[None], jnp.arange(W, dtype=jnp.int32), orders]).astype(jnp.int32)
    block = (None, piece, units)
    shape = (W, piece, units)
    return pl.pallas_call(
        body,
        grid_spec=pltpu.PrefetchScalarGridSpec(
            num_scalar_prefetch=1,
            grid=(W,),
            in_specs=[
                pl.BlockSpec((piece, width), rows_of(True)),
                pl.BlockSpec((piece, width), rows_of(False)),
                pl.BlockSpec((piece, 1), rows_of(True)),
                pl.BlockSpec((piece, 1), rows_of(False)),
                pl.BlockSpec((2, units, width), lambda i, s: (0, 0, 0)),
                pl.BlockSpec((count, units), lambda i, s: (0, 0)),
            ],
            out_specs=[pl.BlockSpec(block, place_at(p)) for p in (0, 1, 0, 1)],
        ),
        out_shape=[jax.ShapeDtypeStruct(shape, d) for d in (BF16, BF16, F32, F32)],
        cost_estimate=pl.CostEstimate(
            flops=4 * W * piece * units * (2 * width + count), bytes_accessed=20 * 2**20, transcendentals=0
        ),
        name="gate_up",
    )(scalars, acts, acts, codes, codes, weights, terms)


def down(orders, ad, mine, theirs, weight):
    _, piece, units = mine.shape
    width = weight.shape[1]
    part, cols = piece // Y, width // 2

    def body(s, m, t, w, held_a, away_a, held_b, away_b, full):
        x = jnp.where(pl.program_id(0) == 0, m[...], t[...])
        full[...] = jnp.dot(x, w[...], preferred_element_type=F32)
        for f, (held, away) in enumerate(((held_a, away_a), (held_b, away_b))):
            for j in range(4):
                at = pl.multiple_of(s[1 + 4 * f + j] * part, 8)
                value = full[pl.ds(at, part), f * cols:(f + 1) * cols]
                if j < 2:
                    held[j] = value
                else:
                    away[j - 2] = value.astype(BF16)

    def at_z(e, i, s):
        return (0, (s[0] ^ e) * W + i, 0, 0)

    spec = pl.BlockSpec((2, None, part, cols), at_z)
    return pl.pallas_call(
        body,
        grid_spec=pltpu.PrefetchScalarGridSpec(
            num_scalar_prefetch=1,
            grid=(2, W),
            in_specs=[
                pl.BlockSpec((None, piece, units), lambda e, i, s: (jnp.where(e == 0, i, W - 1), 0, 0)),
                pl.BlockSpec((None, piece, units), lambda e, i, s: (jnp.where(e == 0, 0, i), 0, 0)),
                pl.BlockSpec((units, width), lambda e, i, s: (0, 0)),
            ],
            out_specs=[spec] * 4,
            scratch_shapes=[pltpu.VMEM((piece, width), F32)],
        ),
        out_shape=[jax.ShapeDtypeStruct((2, Z, part, cols), d) for d in (F32, BF16, F32, BF16)],
        cost_estimate=pl.CostEstimate(
            flops=4 * W * piece * units * width, bytes_accessed=12 * 2**20, transcendentals=0
        ),
        name="down",
    )(jnp.concatenate([ad[None], orders]).astype(jnp.int32), mine, theirs, weight)


def halve(held, away, axis, steps):
    got = lax.ppermute(away, axis, steps[0]).astype(F32)
    later = (held[1] + got[1]).astype(BF16)
    return held[0] + got[0] + lax.ppermute(later, axis, steps[1]).astype(F32)


def local(activations, row_adapter_index, gate_up_weight, down_weight, shrink, expand):
    hid = lax.axis_index(("y", "z"))
    wid = lax.axis_index("wid")
    ad = lax.axis_index("ad")
    n_hid = Y * Z
    total_rows, batches, width = activations.shape
    rows = total_rows * batches
    block = rows // n_hid
    part = block // CHUNKS
    units = down_weight.shape[0]
    rank = shrink.shape[2]
    slots = 2 * n_hid

    by_owner = split_owners(expand[0, 0], n_hid, units)
    by_owner, activations = lax.optimization_barrier((by_owner, activations))
    with jax.named_scope("expand_send"):
        expand_all = send(by_owner, ("y", "z"))

    acts = order_rows(activations)

    def to_chunks(flat):
        return flat.reshape(Y, Z, CHUNKS, part).transpose(2, 1, 0, 3)

    ids = row_adapter_index.reshape(n_hid, block)
    same = ids[:, :, None] == ids[:, None, :]
    earlier = jnp.arange(block)[None, :] < jnp.arange(block)[:, None]
    place = jnp.sum((same & earlier[None]).astype(jnp.int32), axis=2)
    slot = 2 * jnp.arange(n_hid, dtype=jnp.int32)[:, None] + place
    owner, cls = ids // W, ids % W
    send_code = jnp.where(owner == hid, cls * slots + slot, -1)
    recv_code = jnp.where(cls == wid, owner * slots + slot, -1)
    send_code = to_chunks(send_code).reshape(rows)
    recv_code = to_chunks(recv_code).reshape(rows, 1)

    with jax.named_scope("pick"):
        pick = (jnp.arange(W * slots, dtype=jnp.int32)[:, None] == send_code[None, :]).astype(BF16)
        picked = jnp.dot(pick, acts, preferred_element_type=F32).astype(BF16)
    with jax.named_scope("rows_x"):
        mine = rows_x(picked.reshape(W, slots, width))
    with jax.named_scope("rows_ad"):
        theirs = swap(mine)
    first, second = by_core(ad, mine, theirs)
    shrink_blocks = shrink[0, 0].reshape(rank, W, 2, width)
    inner = jnp.einsum("xsf,jxf->sj", first, shrink_blocks[:, :, 0], preferred_element_type=F32)
    inner = inner + jnp.einsum("xsf,jxf->sj", second, shrink_blocks[:, :, 1], preferred_element_type=F32)
    inner, expand_all = lax.optimization_barrier((inner.astype(BF16), expand_all))
    with jax.named_scope("inner_send"):
        inner_all = spread(inner, ("y", "z"), n_hid)
    with jax.named_scope("terms"):
        terms = jnp.einsum(
            "hsj,hju->hsu", inner_all, expand_all, preferred_element_type=F32
        ).astype(BF16).reshape(n_hid * slots, units)

    weights = gate_up_weight.transpose(1, 2, 0)
    x_orders = ring_orders(wid)
    x_places = jnp.concatenate([
        jnp.sum(jnp.where(order[:, None] == jnp.arange(W)[None], jnp.arange(W)[:, None], 0), axis=0)
        for order in x_orders
    ])
    y_orders = jnp.concatenate(ring_orders(lax.axis_index("y")))
    outs = []
    for c in range(CHUNKS):
        away_g, away_u, keep_g, keep_u = gate_up(x_places, ad, acts, recv_code, weights, terms, c)
        with jax.named_scope("gate_send"):
            pair = keep_g + swap(away_g).astype(F32)
            gate = halve(pair[:2], pair[2:].astype(BF16), "wid", (PAIRS, ACROSS))
            pair = keep_u + swap(away_u).astype(F32)
            up = halve(pair[:2], pair[2:].astype(BF16), "wid", (ACROSS, PAIRS))
        hidden = (jax.nn.silu(gate) * up).astype(BF16)
        with jax.named_scope("hidden_send"):
            hidden = spread(hidden, "wid", W)
        held_a, away_a, held_b, away_b = down(y_orders, ad, hidden, swap(hidden), down_weight)
        with jax.named_scope("y_send"):
            low = halve(held_a, away_a, "y", (PAIRS, ACROSS))
            high = halve(held_b, away_b, "y", (ACROSS, PAIRS))
            partial = jnp.concatenate([low.astype(BF16), high.astype(BF16)], axis=-1)
        with jax.named_scope("z_send"):
            partial = jnp.sum(send(partial, "z").astype(F32), axis=0).astype(BF16)
        outs.append(partial)
    out = jnp.concatenate(outs, axis=0)
    return out.reshape(total_rows // n_hid, batches, -1)


def rows_x(blocks):
    me = lax.axis_index("wid")
    full = lax.dynamic_update_index_in_dim(
        jnp.zeros_like(blocks), lax.dynamic_index_in_dim(blocks, me, 0, keepdims=False), me, 0
    )
    for k in (2, 1, 3):
        away = lax.dynamic_index_in_dim(blocks, (me + k) % W, 0, keepdims=False)
        value = lax.ppermute(away, "wid", [(i, (i + k) % W) for i in range(W)])
        full = lax.dynamic_update_index_in_dim(full, value, (me + W - k) % W, 0)
    return full


def solution(mesh):
    grid = Mesh(mesh.devices.reshape(Y, Z, W, 2), ("y", "z", "wid", "ad"))
    hid = ("y", "z")
    in_specs = (
        P(None, None, ("wid", "ad")),
        P(),
        P(("wid", "ad"), None, hid),
        P(hid, ("wid", "ad")),
        P(("y", "z", "wid"), "ad", None, None),
        P(("y", "z", "wid"), "ad", None, None),
    )
    return jax.shard_map(local, mesh=grid, in_specs=in_specs, out_specs=P(hid, None, ("wid", "ad")), check_vma=False)
```

```python
import jax
import jax.numpy as jnp
from jax import lax
from jax.experimental import pallas as pl
from jax.experimental.pallas import tpu as pltpu
from jax.sharding import Mesh, PartitionSpec as P

CHUNKS = 2
Y, Z, W = 4, 8, 4
F32 = jnp.float32
BF16 = jnp.bfloat16
PAIRS = [(i, i ^ 1) for i in range(4)]
ACROSS = [(i, 3 - i) for i in range(4)]


def swap(value):
    return lax.ppermute(value, "ad", [(0, 1), (1, 0)])


def by_core(ad, mine, theirs):
    return jnp.where(ad == 0, mine, theirs), jnp.where(ad == 0, theirs, mine)


def send(blocks, axis):
    return lax.all_to_all(blocks, axis, split_axis=0, concat_axis=0, tiled=True)


def spread(value, axis, n):
    return send(jnp.broadcast_to(value[None], (n,) + value.shape), axis)


def ring_orders(me):
    side, far = me ^ 1, 3 - me
    return jnp.stack([me, far, side, 3 - side]), jnp.stack([me, side, far, far ^ 1])


def split_owners(expand, n, units):
    def body(x, o):
        for h in range(n):
            o[h] = x[:, h * units:(h + 1) * units]

    rank = expand.shape[0]
    return pl.pallas_call(
        body,
        out_shape=jax.ShapeDtypeStruct((n, rank, units), expand.dtype),
        cost_estimate=pl.CostEstimate(flops=0, bytes_accessed=4 * expand.size, transcendentals=0),
        name="split_owners",
    )(expand)


def order_rows(activations):
    total, batches, width = activations.shape
    count = total // (Y * Z * CHUNKS)
    rows = Y * count * batches

    def body(x, o):
        o[...] = x[...].reshape(rows, width)

    return pl.pallas_call(
        body,
        grid=(CHUNKS, Z),
        in_specs=[pl.BlockSpec((Y, None, count, batches, width), lambda c, z: (0, z, c, 0, 0))],
        out_specs=pl.BlockSpec((rows, width), lambda c, z: (c * Z + z, 0)),
        out_shape=jax.ShapeDtypeStruct((total * batches, width), activations.dtype),
        cost_estimate=pl.CostEstimate(flops=0, bytes_accessed=4 * activations.size, transcendentals=0),
        name="order_rows",
    )(activations.reshape(Y, Z, CHUNKS * count, batches, width))


def adapter_terms(inner, expand):
    n, slots, rank = inner.shape
    units = expand.shape[2]
    per = slots // Z
    group = 8

    def body(a, b, o):
        for k in range(0, group, 2):
            two = [
                jnp.dot(a[k + i], b[k + i], preferred_element_type=F32).reshape(Z, per, units) for i in range(2)
            ]
            o[:, k * per:(k + 2) * per, :] = jnp.concatenate(two, axis=1).astype(BF16)

    return pl.pallas_call(
        body,
        grid=(n // group,),
        in_specs=[
            pl.BlockSpec((group, slots, rank), lambda i: (i, 0, 0)),
            pl.BlockSpec((group, rank, units), lambda i: (i, 0, 0)),
        ],
        out_specs=pl.BlockSpec((Z, group * per, units), lambda i: (0, i, 0)),
        out_shape=jax.ShapeDtypeStruct((Z, n * per, units), BF16),
        cost_estimate=pl.CostEstimate(
            flops=2 * n * slots * rank * units, bytes_accessed=4 * expand.size, transcendentals=0
        ),
        name="adapter_terms",
    )(inner, expand)


def gate_up(places, ad, acts, codes, weights, terms, chunk):
    _, units, width = weights.shape
    piece = acts.shape[0] // (CHUNKS * 2 * W)
    count = terms.shape[1]

    def body(s, xa, xk, ca, ck, ta, tk, w, ag, au, kg, ku):
        core = s[0]
        wide = lax.broadcasted_iota(jnp.int32, (piece, count), 1)
        x = jnp.concatenate([xa[...], xk[...]], axis=0)
        extra = jnp.concatenate([
            jnp.dot((c[...] == wide).astype(BF16), t[...], preferred_element_type=F32)
            for c, t in ((ca, ta), (ck, tk))
        ], axis=0).astype(BF16).astype(F32)
        for p, (away, keep) in enumerate(((ag, kg), (au, ku))):
            value = lax.dot_general(x, w[p], (((1,), (1,)), ((), ())), preferred_element_type=F32)
            value = value + jnp.where(core == p, extra, 0.0)
            away[...] = value[:piece].astype(BF16)
            keep[...] = value[piece:]

    def z_of(away, i, s):
        return (1 - s[0] if away else s[0]) * W + i

    def rows_of(away):
        return lambda i, s: (chunk * 2 * W + z_of(away, i, s), 0)

    def terms_of(away):
        return lambda i, s: (z_of(away, i, s), 0, 0)

    def place_at(p):
        return lambda i, s: (s[1 + W * p + i], 0, 0)

    scalars = jnp.concatenate([ad[None], places]).astype(jnp.int32)
    block = (None, piece, units)
    shape = (W, piece, units)
    return pl.pallas_call(
        body,
        grid_spec=pltpu.PrefetchScalarGridSpec(
            num_scalar_prefetch=1,
            grid=(W,),
            in_specs=[
                pl.BlockSpec((piece, width), rows_of(True)),
                pl.BlockSpec((piece, width), rows_of(False)),
                pl.BlockSpec((piece, 1), rows_of(True)),
                pl.BlockSpec((piece, 1), rows_of(False)),
                pl.BlockSpec((None, count, units), terms_of(True)),
                pl.BlockSpec((None, count, units), terms_of(False)),
                pl.BlockSpec((2, units, width), lambda i, s: (0, 0, 0)),
            ],
            out_specs=[pl.BlockSpec(block, place_at(p)) for p in (0, 1, 0, 1)],
        ),
        out_shape=[jax.ShapeDtypeStruct(shape, d) for d in (BF16, BF16, F32, F32)],
        cost_estimate=pl.CostEstimate(
            flops=4 * W * piece * units * (2 * width + count), bytes_accessed=16 * 2**20, transcendentals=0
        ),
        name="gate_up",
    )(scalars, acts, acts, codes, codes, terms, terms, weights)


def down(orders, ad, mine, theirs, weight):
    _, piece, units = mine.shape
    width = weight.shape[1]
    part, cols = piece // Y, width // 2

    def body(s, m, t, w, held_a, away_a, held_b, away_b, full):
        x = jnp.where(pl.program_id(0) == 0, m[...], t[...]).reshape(W * piece, units)
        full[...] = jnp.dot(x, w[...], preferred_element_type=F32).reshape(W, piece, width)
        for f, (held, away) in enumerate(((held_a, away_a), (held_b, away_b))):
            for j in range(4):
                at = pl.multiple_of(s[1 + 4 * f + j] * part, 8)
                for i in range(W):
                    value = full[i, pl.ds(at, part), f * cols:(f + 1) * cols]
                    if j < 2:
                        held[j, i] = value
                    else:
                        away[j - 2, i] = value.astype(BF16)

    spec = pl.BlockSpec((2, W, part, cols), lambda e, s: (0, s[0] ^ e, 0, 0))
    whole = pl.BlockSpec((W, piece, units), lambda e, s: (0, 0, 0))
    return pl.pallas_call(
        body,
        grid_spec=pltpu.PrefetchScalarGridSpec(
            num_scalar_prefetch=1,
            grid=(2,),
            in_specs=[whole, whole, pl.BlockSpec((units, width), lambda e, s: (0, 0))],
            out_specs=[spec] * 4,
            scratch_shapes=[pltpu.VMEM((W, piece, width), F32)],
        ),
        out_shape=[jax.ShapeDtypeStruct((2, Z, part, cols), d) for d in (F32, BF16, F32, BF16)],
        cost_estimate=pl.CostEstimate(
            flops=4 * W * piece * units * width, bytes_accessed=12 * 2**20, transcendentals=0
        ),
        name="down",
    )(jnp.concatenate([ad[None], orders]).astype(jnp.int32), mine, theirs, weight)


def first_step(held, others, axis, steps):
    away = (held[2:] + others[2:].astype(F32)).astype(BF16)
    return lax.ppermute(away, axis, steps[0])


def last_step(held, got, axis, steps):
    later = (held(1) + got[1].astype(F32)).astype(BF16)
    return held(0) + got[0].astype(F32) + lax.ppermute(later, axis, steps[1]).astype(F32)


def local(activations, row_adapter_index, gate_up_weight, down_weight, shrink, expand):
    hid = lax.axis_index(("y", "z"))
    wid = lax.axis_index("wid")
    ad = lax.axis_index("ad")
    n_hid = Y * Z
    total_rows, batches, width = activations.shape
    rows = total_rows * batches
    block = rows // n_hid
    part = block // CHUNKS
    units = down_weight.shape[0]
    rank = shrink.shape[2]
    slots = 2 * n_hid

    by_owner = split_owners(expand[0, 0], n_hid, units)
    by_owner, activations = lax.optimization_barrier((by_owner, activations))
    with jax.named_scope("expand_send"):
        expand_all = send(by_owner, ("y", "z"))

    acts = order_rows(activations)

    def to_chunks(flat):
        return flat.reshape(Y, Z, CHUNKS, part).transpose(2, 1, 0, 3)

    ids = row_adapter_index.reshape(n_hid, block)
    same = ids[:, :, None] == ids[:, None, :]
    earlier = jnp.arange(block)[None, :] < jnp.arange(block)[:, None]
    place = jnp.sum((same & earlier[None]).astype(jnp.int32), axis=2)
    member = jnp.arange(n_hid, dtype=jnp.int32)[:, None]
    near = 2 * (member // Z) + place
    slot = 2 * Y * (member % Z) + near
    owner, cls = ids // W, ids % W
    send_code = jnp.where(owner == hid, cls * slots + slot, -1)
    recv_code = jnp.where(cls == wid, 2 * Y * owner + near, -1)
    send_code = to_chunks(send_code).reshape(rows)
    recv_code = to_chunks(recv_code).reshape(rows, 1)

    with jax.named_scope("pick"):
        pick = (jnp.arange(W * slots, dtype=jnp.int32)[:, None] == send_code[None, :]).astype(BF16)
        picked = jnp.dot(pick, acts, preferred_element_type=F32).astype(BF16)
    with jax.named_scope("rows_x"):
        mine = rows_x(picked.reshape(W, slots, width))
    with jax.named_scope("rows_ad"):
        theirs = swap(mine)
    first, second = by_core(ad, mine, theirs)
    shrink_blocks = shrink[0, 0].reshape(rank, W, 2, width)
    inner = jnp.einsum("xsf,jxf->sj", first, shrink_blocks[:, :, 0], preferred_element_type=F32)
    inner = inner + jnp.einsum("xsf,jxf->sj", second, shrink_blocks[:, :, 1], preferred_element_type=F32)
    inner, expand_all = lax.optimization_barrier((inner.astype(BF16), expand_all))
    with jax.named_scope("inner_send"):
        inner_all = spread(inner, ("y", "z"), n_hid)
    with jax.named_scope("terms"):
        terms = adapter_terms(inner_all, expand_all)

    weights = gate_up_weight.transpose(1, 2, 0)
    x_orders = ring_orders(wid)
    x_places = jnp.concatenate([
        jnp.sum(jnp.where(order[:, None] == jnp.arange(W)[None], jnp.arange(W)[:, None], 0), axis=0)
        for order in x_orders
    ])
    y_orders = jnp.concatenate(ring_orders(lax.axis_index("y")))
    low_steps, high_steps = (PAIRS, ACROSS), (ACROSS, PAIRS)

    def start(c):
        away_g, away_u, keep_g, keep_u = gate_up(x_places, ad, acts, recv_code, weights, terms, c)
        with jax.named_scope("gate_send"):
            other_g, other_u = swap(away_g), swap(away_u)
            got_g = first_step(keep_g, other_g, "wid", low_steps)
            got_u = first_step(keep_u, other_u, "wid", high_steps)
        return keep_g, keep_u, other_g, other_u, got_g, got_u

    def finish(keep_g, keep_u, other_g, other_u, got_g, got_u):
        with jax.named_scope("gate_send"):
            gate = last_step(lambda j: keep_g[j] + other_g[j].astype(F32), got_g, "wid", low_steps)
            up = last_step(lambda j: keep_u[j] + other_u[j].astype(F32), got_u, "wid", high_steps)
        hidden = (jax.nn.silu(gate) * up).astype(BF16)
        with jax.named_scope("hidden_send"):
            hidden = spread(hidden, "wid", W)
        return down(y_orders, ad, hidden, swap(hidden), down_weight)

    outs = []
    state = start(0)
    for c in range(CHUNKS):
        later = start(c + 1) if c + 1 < CHUNKS else None
        held_a, away_a, held_b, away_b = finish(*state)
        if later is not None:
            held_a, got_g, got_u = lax.optimization_barrier((held_a, later[4], later[5]))
            state = later[:4] + (got_g, got_u)
        with jax.named_scope("y_send"):
            got_a = lax.ppermute(away_a, "y", low_steps[0])
            got_b = lax.ppermute(away_b, "y", high_steps[0])
            low = last_step(lambda j: held_a[j], got_a, "y", low_steps)
            high = last_step(lambda j: held_b[j], got_b, "y", high_steps)
            partial = jnp.concatenate([low.astype(BF16), high.astype(BF16)], axis=-1)
        with jax.named_scope("z_send"):
            partial = jnp.sum(send(partial, "z").astype(F32), axis=0).astype(BF16)
        outs.append(partial)
    out = jnp.concatenate(outs, axis=0)
    return out.reshape(total_rows // n_hid, batches, -1)


def rows_x(blocks):
    me = lax.axis_index("wid")
    full = lax.dynamic_update_index_in_dim(
        jnp.zeros_like(blocks), lax.dynamic_index_in_dim(blocks, me, 0, keepdims=False), me, 0
    )
    for k in (2, 1, 3):
        away = lax.dynamic_index_in_dim(blocks, (me + k) % W, 0, keepdims=False)
        value = lax.ppermute(away, "wid", [(i, (i + k) % W) for i in range(W)])
        full = lax.dynamic_update_index_in_dim(full, value, (me + W - k) % W, 0)
    return full


def solution(mesh):
    grid = Mesh(mesh.devices.reshape(Y, Z, W, 2), ("y", "z", "wid", "ad"))
    hid = ("y", "z")
    in_specs = (
        P(None, None, ("wid", "ad")),
        P(),
        P(("wid", "ad"), None, hid),
        P(hid, ("wid", "ad")),
        P(("y", "z", "wid"), "ad", None, None),
        P(("y", "z", "wid"), "ad", None, None),
    )
    return jax.shard_map(local, mesh=grid, in_specs=in_specs, out_specs=P(hid, None, ("wid", "ad")), check_vma=False)
```

```python
import jax
import jax.numpy as jnp
from jax import lax
from jax.experimental import pallas as pl
from jax.experimental.pallas import tpu as pltpu
from jax.sharding import Mesh, PartitionSpec as P


CHUNKS = 2
Y, Z, W = 4, 8, 4
F32 = jnp.float32
BF16 = jnp.bfloat16
PAIRS = [(i, i ^ 1) for i in range(4)]
ACROSS = [(i, 3 - i) for i in range(4)]


def swap(value):
    return lax.ppermute(value, "ad", [(0, 1), (1, 0)])


def by_core(ad, mine, theirs):
    return jnp.where(ad == 0, mine, theirs), jnp.where(ad == 0, theirs, mine)


def send(blocks, axis):
    return lax.all_to_all(blocks, axis, split_axis=0, concat_axis=0, tiled=True)


def spread(value, axis, n):
    return send(jnp.broadcast_to(value[None], (n,) + value.shape), axis)


def ring_orders(me):
    side, far = me ^ 1, 3 - me
    return jnp.stack([me, far, side, 3 - side]), jnp.stack([me, side, far, far ^ 1])


def split_owners(expand, n, units):
    def body(x, o):
        for h in range(n):
            o[h] = x[:, h * units:(h + 1) * units]

    rank = expand.shape[0]
    return pl.pallas_call(
        body,
        out_shape=jax.ShapeDtypeStruct((n, rank, units), expand.dtype),
        cost_estimate=pl.CostEstimate(flops=0, bytes_accessed=4 * expand.size, transcendentals=0),
        name="split_owners",
    )(expand)


def order_rows(activations):
    total, batches, width = activations.shape
    count = total // (Y * Z * CHUNKS)
    rows = Y * count * batches

    def body(x, o):
        o[...] = x[...].reshape(rows, width)

    return pl.pallas_call(
        body,
        grid=(CHUNKS, Z),
        in_specs=[pl.BlockSpec((Y, None, count, batches, width), lambda c, z: (0, z, c, 0, 0))],
        out_specs=pl.BlockSpec((rows, width), lambda c, z: (c * Z + z, 0)),
        out_shape=jax.ShapeDtypeStruct((total * batches, width), activations.dtype),
        cost_estimate=pl.CostEstimate(flops=0, bytes_accessed=4 * activations.size, transcendentals=0),
        name="order_rows",
    )(activations.reshape(Y, Z, CHUNKS * count, batches, width))


def adapter_terms(member, inner, expand):
    _, slots, rank = inner.shape
    units = expand.shape[2]
    per = slots // Z

    def body(s, a, b, o):
        for j in range(0, Y, 2):
            two = [
                jnp.dot(a[j + i], b[s[0] ^ (j + i)], preferred_element_type=F32).reshape(Z, per, units)
                for i in range(2)
            ]
            o[:, j * per:(j + 2) * per, :] = jnp.concatenate(two, axis=1).astype(BF16)

    return pl.pallas_call(
        body,
        grid_spec=pltpu.PrefetchScalarGridSpec(
            num_scalar_prefetch=1,
            grid=(Z,),
            in_specs=[
                pl.BlockSpec((Y, slots, rank), lambda i, s: (i, 0, 0)),
                pl.BlockSpec((Y, None, rank, units), lambda i, s: (0, s[1] ^ i, 0, 0)),
            ],
            out_specs=pl.BlockSpec((Z, Y * per, units), lambda i, s: (0, i, 0)),
        ),
        out_shape=jax.ShapeDtypeStruct((Z, Y * Z * per, units), BF16),
        cost_estimate=pl.CostEstimate(
            flops=2 * Y * Z * slots * rank * units, bytes_accessed=4 * expand.size, transcendentals=0
        ),
        name="adapter_terms",
    )(member, inner, expand.reshape(Y, Z, rank, units))


def gate_up(places, ad, acts, codes, weights, terms, chunk):
    _, width, units = weights.shape
    piece = acts.shape[0] // (CHUNKS * 2 * W)
    count = terms.shape[1]

    def body(s, xa, xk, ca, ck, ta, tk, w, ag, au, kg, ku):
        core = s[0]
        wide = lax.broadcasted_iota(jnp.int32, (piece, count), 1)
        x = jnp.concatenate([xa[...], xk[...]], axis=0)
        extra = jnp.concatenate([
            jnp.dot((c[...] == wide).astype(BF16), t[...], preferred_element_type=F32)
            for c, t in ((ca, ta), (ck, tk))
        ], axis=0).astype(BF16).astype(F32)
        for p, (away, keep) in enumerate(((ag, kg), (au, ku))):
            value = jnp.dot(x, w[p], preferred_element_type=F32) + jnp.where(core == p, extra, 0.0)
            away[...] = value[:piece].astype(BF16)
            keep[...] = value[piece:]

    def z_of(away, i, s):
        return (1 - s[0] if away else s[0]) * W + i

    def rows_of(away):
        return lambda i, s: (chunk * 2 * W + z_of(away, i, s), 0)

    def terms_of(away):
        return lambda i, s: (z_of(away, i, s), 0, 0)

    def place_at(p):
        return lambda i, s: (s[1 + W * p + i], 0, 0)

    scalars = jnp.concatenate([ad[None], places]).astype(jnp.int32)
    block = (None, piece, units)
    shape = (W, piece, units)
    return pl.pallas_call(
        body,
        grid_spec=pltpu.PrefetchScalarGridSpec(
            num_scalar_prefetch=1,
            grid=(W,),
            in_specs=[
                pl.BlockSpec((piece, width), rows_of(True)),
                pl.BlockSpec((piece, width), rows_of(False)),
                pl.BlockSpec((piece, 1), rows_of(True)),
                pl.BlockSpec((piece, 1), rows_of(False)),
                pl.BlockSpec((None, count, units), terms_of(True)),
                pl.BlockSpec((None, count, units), terms_of(False)),
                pl.BlockSpec((2, width, units), lambda i, s: (0, 0, 0)),
            ],
            out_specs=[pl.BlockSpec(block, place_at(p)) for p in (0, 1, 0, 1)],
        ),
        out_shape=[jax.ShapeDtypeStruct(shape, d) for d in (BF16, BF16, F32, F32)],
        cost_estimate=pl.CostEstimate(
            flops=4 * W * piece * units * (2 * width + count), bytes_accessed=16 * 2**20, transcendentals=0
        ),
        name="gate_up",
    )(scalars, acts, acts, codes, codes, terms, terms, weights)


def down(orders, ad, mine, theirs, weight):
    _, piece, units = mine.shape
    width = weight.shape[1]
    part, cols = piece // Y, width // 2

    def body(s, m, t, w, held_a, away_a, held_b, away_b, full):
        x = jnp.where(pl.program_id(0) == 0, m[...], t[...]).reshape(W * piece, units)
        full[...] = jnp.dot(x, w[...], preferred_element_type=F32).reshape(W, piece, width)
        for f, (held, away) in enumerate(((held_a, away_a), (held_b, away_b))):
            for j in range(4):
                at = pl.multiple_of(s[1 + 4 * f + j] * part, 8)
                for i in range(W):
                    value = full[i, pl.ds(at, part), f * cols:(f + 1) * cols]
                    if j < 2:
                        held[j, i] = value
                    else:
                        away[j - 2, i] = value.astype(BF16)

    spec = pl.BlockSpec((2, W, part, cols), lambda e, s: (0, s[0] ^ e, 0, 0))
    whole = pl.BlockSpec((W, piece, units), lambda e, s: (0, 0, 0))
    return pl.pallas_call(
        body,
        grid_spec=pltpu.PrefetchScalarGridSpec(
            num_scalar_prefetch=1,
            grid=(2,),
            in_specs=[whole, whole, pl.BlockSpec((units, width), lambda e, s: (0, 0))],
            out_specs=[spec] * 4,
            scratch_shapes=[pltpu.VMEM((W, piece, width), F32)],
        ),
        out_shape=[jax.ShapeDtypeStruct((2, Z, part, cols), d) for d in (F32, BF16, F32, BF16)],
        cost_estimate=pl.CostEstimate(
            flops=4 * W * piece * units * width, bytes_accessed=12 * 2**20, transcendentals=0
        ),
        name="down",
    )(jnp.concatenate([ad[None], orders]).astype(jnp.int32), mine, theirs, weight)


def first_step(held, others, axis, steps):
    away = (held[2:] + others[2:].astype(F32)).astype(BF16)
    return lax.ppermute(away, axis, steps[0])


def last_step(held, got, axis, steps):
    later = (held(1) + got[1].astype(F32)).astype(BF16)
    return held(0) + got[0].astype(F32) + lax.ppermute(later, axis, steps[1]).astype(F32)


def layer(activations, row_adapter_index, gate_up_weight, down_weight, shrink, expand):
    hid = lax.axis_index(("y", "z"))
    wid = lax.axis_index("wid")
    ad = lax.axis_index("ad")
    my_y, my_z = lax.axis_index("y"), lax.axis_index("z")
    n_hid = Y * Z
    total_rows, batches, width = activations.shape
    rows = total_rows * batches
    block = rows // n_hid
    part = block // CHUNKS
    units = down_weight.shape[0]
    rank = shrink.shape[2]
    slots = 2 * n_hid

    by_owner = split_owners(expand[0, 0], n_hid, units)
    by_owner, activations = lax.optimization_barrier((by_owner, activations))
    expand_all = send(by_owner, ("y", "z"))

    acts = order_rows(activations)

    def to_chunks(flat):
        return flat.reshape(Y, Z, CHUNKS, part).transpose(2, 1, 0, 3)

    ids = row_adapter_index.reshape(n_hid, block)
    same = ids[:, :, None] == ids[:, None, :]
    earlier = jnp.arange(block)[None, :] < jnp.arange(block)[:, None]
    place = jnp.sum((same & earlier[None]).astype(jnp.int32), axis=2)
    member = jnp.arange(n_hid, dtype=jnp.int32)[:, None]
    near = 2 * (member // Z) + place
    slot = 2 * Y * (member % Z) + near
    owner, cls = ids // W, ids % W
    send_code = jnp.where(owner == hid, cls * slots + slot, -1)
    recv_code = jnp.where(cls == wid, 2 * Y * (Y * (owner % Z ^ my_z) + (owner // Z ^ my_y)) + near, -1)
    send_code = to_chunks(send_code).reshape(rows)
    recv_code = to_chunks(recv_code).reshape(rows, 1)

    pick = (jnp.arange(W * slots, dtype=jnp.int32)[:, None] == send_code[None, :]).astype(BF16)
    picked = jnp.dot(pick, acts, preferred_element_type=F32).astype(BF16)
    mine = rows_x(picked.reshape(W, slots, width))
    theirs = swap(mine)
    first, second = by_core(ad, mine, theirs)
    shrink_blocks = shrink[0, 0].reshape(rank, W, 2, width)
    inner = jnp.einsum("xsf,jxf->sj", first, shrink_blocks[:, :, 0], preferred_element_type=F32)
    inner = inner + jnp.einsum("xsf,jxf->sj", second, shrink_blocks[:, :, 1], preferred_element_type=F32)
    inner_all = inner.astype(BF16)[None]
    for axis, n in (("y", Y), ("z", Z)):
        for bit in range(n.bit_length() - 1):
            got = lax.ppermute(inner_all, axis, [(i, i ^ (1 << bit)) for i in range(n)])
            inner_all = jnp.concatenate([inner_all, got], axis=0)
    terms = adapter_terms(jnp.stack([my_y, my_z]).astype(jnp.int32), inner_all, expand_all)

    weights = gate_up_weight.transpose(1, 0, 2)
    x_orders = ring_orders(wid)
    x_places = jnp.concatenate([
        jnp.sum(jnp.where(order[:, None] == jnp.arange(W)[None], jnp.arange(W)[:, None], 0), axis=0)
        for order in x_orders
    ])
    y_orders = jnp.concatenate(ring_orders(lax.axis_index("y")))
    low_steps, high_steps = (PAIRS, ACROSS), (ACROSS, PAIRS)

    def start(c):
        away_g, away_u, keep_g, keep_u = gate_up(x_places, ad, acts, recv_code, weights, terms, c)
        other_g, other_u = swap(away_g), swap(away_u)
        got_g = first_step(keep_g, other_g, "wid", low_steps)
        got_u = first_step(keep_u, other_u, "wid", high_steps)
        return keep_g, keep_u, other_g, other_u, got_g, got_u

    def finish(keep_g, keep_u, other_g, other_u, got_g, got_u):
        gate = last_step(lambda j: keep_g[j] + other_g[j].astype(F32), got_g, "wid", low_steps)
        up = last_step(lambda j: keep_u[j] + other_u[j].astype(F32), got_u, "wid", high_steps)
        hidden = (jax.nn.silu(gate) * up).astype(BF16)
        hidden = spread(hidden, "wid", W)
        theirs = swap(hidden)
        return down(y_orders, ad, hidden, theirs, down_weight)

    outs = []
    state = start(0)
    for c in range(CHUNKS):
        later = start(c + 1) if c + 1 < CHUNKS else None
        held_a, away_a, held_b, away_b = finish(*state)
        if later is not None:
            held_a, got_g, got_u = lax.optimization_barrier((held_a, later[4], later[5]))
            state = later[:4] + (got_g, got_u)
        got_a = lax.ppermute(away_a, "y", low_steps[0])
        got_b = lax.ppermute(away_b, "y", high_steps[0])
        low = last_step(lambda j: held_a[j], got_a, "y", low_steps)
        high = last_step(lambda j: held_b[j], got_b, "y", high_steps)
        partial = jnp.concatenate([low.astype(BF16), high.astype(BF16)], axis=-1)
        partial = jnp.sum(send(partial, "z").astype(F32), axis=0).astype(BF16)
        outs.append(partial)
    out = jnp.concatenate(outs, axis=0)
    return out.reshape(total_rows // n_hid, batches, -1)


def rows_x(blocks):
    me = lax.axis_index("wid")
    full = lax.dynamic_update_index_in_dim(
        jnp.zeros_like(blocks), lax.dynamic_index_in_dim(blocks, me, 0, keepdims=False), me, 0
    )
    for k in (2, 1, 3):
        away = lax.dynamic_index_in_dim(blocks, (me + k) % W, 0, keepdims=False)
        value = lax.ppermute(away, "wid", [(i, (i + k) % W) for i in range(W)])
        full = lax.dynamic_update_index_in_dim(full, value, (me + W - k) % W, 0)
    return full


def solution(mesh):
    grid = Mesh(mesh.devices.reshape(Y, Z, W, 2), ("y", "z", "wid", "ad"))
    hid = ("y", "z")
    in_specs = (
        P(None, None, ("wid", "ad")),
        P(),
        P(("wid", "ad"), None, hid),
        P(hid, ("wid", "ad")),
        P(("y", "z", "wid"), "ad", None, None),
        P(("y", "z", "wid"), "ad", None, None),
    )
    return jax.shard_map(
        layer, mesh=grid, in_specs=in_specs, out_specs=P(hid, None, ("wid", "ad")), check_vma=False
    )
```

```python
import jax
import jax.numpy as jnp
from jax import lax
from jax.experimental import pallas as pl
from jax.experimental.pallas import tpu as pltpu
from jax.sharding import Mesh, PartitionSpec as P


CHUNKS = 3
Y, Z, W = 4, 8, 4
F32 = jnp.float32
BF16 = jnp.bfloat16
PAIRS = [(i, i ^ 1) for i in range(4)]
ACROSS = [(i, 3 - i) for i in range(4)]


def swap(value):
    return lax.ppermute(value, "ad", [(0, 1), (1, 0)])


def by_core(ad, mine, theirs):
    return jnp.where(ad == 0, mine, theirs), jnp.where(ad == 0, theirs, mine)


def send(blocks, axis):
    return lax.all_to_all(blocks, axis, split_axis=0, concat_axis=0, tiled=True)


def spread(value, axis, n):
    return send(jnp.broadcast_to(value[None], (n,) + value.shape), axis)


def ring_orders(me):
    side, far = me ^ 1, 3 - me
    return jnp.stack([me, far, side, 3 - side]), jnp.stack([me, side, far, far ^ 1])


def split_owners(expand, n, units):
    def body(x, o):
        for h in range(n):
            o[h] = x[:, h * units:(h + 1) * units]

    rank = expand.shape[0]
    return pl.pallas_call(
        body,
        out_shape=jax.ShapeDtypeStruct((n, rank, units), expand.dtype),
        cost_estimate=pl.CostEstimate(flops=0, bytes_accessed=4 * expand.size, transcendentals=0),
        name="split_owners",
    )(expand)


def order_rows(activations):
    total, batches, width = activations.shape
    count = total // (Y * Z * CHUNKS)
    rows = Y * count * batches

    def body(x, o):
        o[...] = x[...].reshape(rows, width)

    return pl.pallas_call(
        body,
        grid=(CHUNKS, Z),
        in_specs=[pl.BlockSpec((Y, None, count, batches, width), lambda c, z: (0, z, c, 0, 0))],
        out_specs=pl.BlockSpec((rows, width), lambda c, z: (c * Z + z, 0)),
        out_shape=jax.ShapeDtypeStruct((total * batches, width), activations.dtype),
        cost_estimate=pl.CostEstimate(flops=0, bytes_accessed=4 * activations.size, transcendentals=0),
        name="order_rows",
    )(activations.reshape(Y, Z, CHUNKS * count, batches, width))


def adapter_terms(my_y, inner, expand):
    _, _, slots, rank = inner.shape
    units = expand.shape[2]
    per = slots // Z
    group = 2

    def body(s, a, b, o):
        for k in range(group):
            for j in range(0, Y, 2):
                two = [
                    jnp.dot(a[k, j + i], b[s[0] ^ (j + i), k], preferred_element_type=F32).reshape(Z, per, units)
                    for i in range(2)
                ]
                at = (k * Y + j) * per
                o[:, at:at + 2 * per, :] = jnp.concatenate(two, axis=1).astype(BF16)

    return pl.pallas_call(
        body,
        grid_spec=pltpu.PrefetchScalarGridSpec(
            num_scalar_prefetch=1,
            grid=(Z // group,),
            in_specs=[
                pl.BlockSpec((group, Y, slots, rank), lambda i, s: (i, 0, 0, 0)),
                pl.BlockSpec((Y, group, rank, units), lambda i, s: (0, i, 0, 0)),
            ],
            out_specs=pl.BlockSpec((Z, group * Y * per, units), lambda i, s: (0, i, 0)),
        ),
        out_shape=jax.ShapeDtypeStruct((Z, Y * Z * per, units), BF16),
        cost_estimate=pl.CostEstimate(
            flops=2 * Y * Z * slots * rank * units, bytes_accessed=4 * expand.size, transcendentals=0
        ),
        name="adapter_terms",
    )(my_y, inner, expand.reshape(Y, Z, rank, units))


def gate_up(places, ad, acts, codes, weights, terms, chunk):
    _, units, width = weights.shape
    piece = acts.shape[0] // (CHUNKS * 2 * W)
    count = terms.shape[1]

    def body(s, xa, xk, ca, ck, ta, tk, w, ag, au, kg, ku):
        core = s[0]
        wide = lax.broadcasted_iota(jnp.int32, (piece, count), 1)
        x = jnp.concatenate([xa[...], xk[...]], axis=0)
        extra = jnp.concatenate([
            jnp.dot((c[...] == wide).astype(BF16), t[...], preferred_element_type=F32)
            for c, t in ((ca, ta), (ck, tk))
        ], axis=0).astype(BF16).astype(F32)
        for p, (away, keep) in enumerate(((ag, kg), (au, ku))):
            value = lax.dot_general(x, w[p], (((1,), (1,)), ((), ())), preferred_element_type=F32) + jnp.where(core == p, extra, 0.0)
            away[...] = value[:piece].astype(BF16)
            keep[...] = value[piece:]

    def z_of(away, i, s):
        return (1 - s[0] if away else s[0]) * W + i

    def rows_of(away):
        return lambda i, s: (chunk * 2 * W + z_of(away, i, s), 0)

    def terms_of(away):
        return lambda i, s: (z_of(away, i, s), 0, 0)

    def place_at(p):
        return lambda i, s: (s[1 + W * p + i], 0, 0)

    scalars = jnp.concatenate([ad[None], places]).astype(jnp.int32)
    block = (None, piece, units)
    shape = (W, piece, units)
    return pl.pallas_call(
        body,
        grid_spec=pltpu.PrefetchScalarGridSpec(
            num_scalar_prefetch=1,
            grid=(W,),
            in_specs=[
                pl.BlockSpec((piece, width), rows_of(True)),
                pl.BlockSpec((piece, width), rows_of(False)),
                pl.BlockSpec((piece, 1), rows_of(True)),
                pl.BlockSpec((piece, 1), rows_of(False)),
                pl.BlockSpec((None, count, units), terms_of(True)),
                pl.BlockSpec((None, count, units), terms_of(False)),
                pl.BlockSpec((2, units, width), lambda i, s: (0, 0, 0)),
            ],
            out_specs=[pl.BlockSpec(block, place_at(p)) for p in (0, 1, 0, 1)],
        ),
        out_shape=[jax.ShapeDtypeStruct(shape, d) for d in (BF16, BF16, F32, F32)],
        cost_estimate=pl.CostEstimate(
            flops=4 * W * piece * units * (2 * width + count), bytes_accessed=16 * 2**20, transcendentals=0
        ),
        name="gate_up",
    )(scalars, acts, acts, codes, codes, terms, terms, weights)


def down(orders, ad, mine, theirs, weight):
    _, piece, units = mine.shape
    width = weight.shape[1]
    part, cols = piece // Y, width // 2

    def body(s, m, t, w, held_a, away_a, held_b, away_b, full):
        x = jnp.where(pl.program_id(0) == 0, m[...], t[...]).reshape(W * piece, units)
        full[...] = jnp.dot(x, w[...], preferred_element_type=F32).reshape(W, piece, width)
        for f, (held, away) in enumerate(((held_a, away_a), (held_b, away_b))):
            for j in range(4):
                at = pl.multiple_of(s[1 + 4 * f + j] * part, 8)
                for i in range(W):
                    value = full[i, pl.ds(at, part), f * cols:(f + 1) * cols]
                    if j < 2:
                        held[j, i] = value
                    else:
                        away[j - 2, i] = value.astype(BF16)

    spec = pl.BlockSpec((2, W, part, cols), lambda e, s: (0, s[0] ^ e, 0, 0))
    whole = pl.BlockSpec((W, piece, units), lambda e, s: (0, 0, 0))
    return pl.pallas_call(
        body,
        grid_spec=pltpu.PrefetchScalarGridSpec(
            num_scalar_prefetch=1,
            grid=(2,),
            in_specs=[whole, whole, pl.BlockSpec((units, width), lambda e, s: (0, 0))],
            out_specs=[spec] * 4,
            scratch_shapes=[pltpu.VMEM((W, piece, width), F32)],
        ),
        out_shape=[jax.ShapeDtypeStruct((2, Z, part, cols), d) for d in (F32, BF16, F32, BF16)],
        cost_estimate=pl.CostEstimate(
            flops=4 * W * piece * units * width, bytes_accessed=12 * 2**20, transcendentals=0
        ),
        name="down",
    )(jnp.concatenate([ad[None], orders]).astype(jnp.int32), mine, theirs, weight)


def first_step(held, others, axis, steps):
    away = (held[2:] + others[2:].astype(F32)).astype(BF16)
    return lax.ppermute(away, axis, steps[0])


def last_step(held, got, axis, steps):
    later = (held(1) + got[1].astype(F32)).astype(BF16)
    return held(0) + got[0].astype(F32) + lax.ppermute(later, axis, steps[1]).astype(F32)


def layer(activations, row_adapter_index, gate_up_weight, down_weight, shrink, expand):
    hid = lax.axis_index(("y", "z"))
    wid = lax.axis_index("wid")
    ad = lax.axis_index("ad")
    my_y = lax.axis_index("y")
    n_hid = Y * Z
    total_rows, batches, width = activations.shape
    rows = total_rows * batches
    block = rows // n_hid
    part = block // CHUNKS
    units = down_weight.shape[0]
    rank = shrink.shape[2]
    slots = 2 * n_hid

    by_owner = split_owners(expand[0, 0], n_hid, units)
    by_owner, activations = lax.optimization_barrier((by_owner, activations))
    expand_all = send(by_owner, ("y", "z"))

    acts = order_rows(activations)

    def to_chunks(flat):
        return flat.reshape(Y, Z, CHUNKS, part).transpose(2, 1, 0, 3)

    ids = row_adapter_index.reshape(n_hid, block)
    same = ids[:, :, None] == ids[:, None, :]
    earlier = jnp.arange(block)[None, :] < jnp.arange(block)[:, None]
    place = jnp.sum((same & earlier[None]).astype(jnp.int32), axis=2)
    member = jnp.arange(n_hid, dtype=jnp.int32)[:, None]
    near = 2 * (member // Z) + place
    slot = 2 * Y * (member % Z) + near
    owner, cls = ids // W, ids % W
    send_code = jnp.where(owner == hid, cls * slots + slot, -1)
    recv_code = jnp.where(cls == wid, 2 * Y * (Y * (owner % Z) + (owner // Z ^ my_y)) + near, -1)
    send_code = to_chunks(send_code).reshape(rows)
    recv_code = to_chunks(recv_code).reshape(rows, 1)

    pick = (jnp.arange(W * slots, dtype=jnp.int32)[:, None] == send_code[None, :]).astype(BF16)
    picked = jnp.dot(pick, acts, preferred_element_type=F32).astype(BF16)
    mine = rows_x(picked.reshape(W, slots, width))
    theirs = swap(mine)
    first, second = by_core(ad, mine, theirs)
    shrink_blocks = shrink[0, 0].reshape(rank, W, 2, width)
    inner = jnp.einsum("xsf,jxf->sj", first, shrink_blocks[:, :, 0], preferred_element_type=F32)
    inner = inner + jnp.einsum("xsf,jxf->sj", second, shrink_blocks[:, :, 1], preferred_element_type=F32)
    inner_all = inner.astype(BF16)[None]
    for bit in range(2):
        got = lax.ppermute(inner_all, "y", [(i, i ^ (1 << bit)) for i in range(Y)])
        inner_all = jnp.concatenate([inner_all, got], axis=0)
    inner_all, expand_all = lax.optimization_barrier((inner_all, expand_all))
    inner_all = spread(inner_all, "z", Z)
    terms = adapter_terms(my_y[None].astype(jnp.int32), inner_all, expand_all)

    weights = gate_up_weight.transpose(1, 2, 0)
    x_orders = ring_orders(wid)
    x_places = jnp.concatenate([
        jnp.sum(jnp.where(order[:, None] == jnp.arange(W)[None], jnp.arange(W)[:, None], 0), axis=0)
        for order in x_orders
    ])
    y_orders = jnp.concatenate(ring_orders(lax.axis_index("y")))
    low_steps, high_steps = (PAIRS, ACROSS), (ACROSS, PAIRS)

    def start(c):
        away_g, away_u, keep_g, keep_u = gate_up(x_places, ad, acts, recv_code, weights, terms, c)
        other_g, other_u = swap(away_g), swap(away_u)
        got_g = first_step(keep_g, other_g, "wid", low_steps)
        got_u = first_step(keep_u, other_u, "wid", high_steps)
        return keep_g, keep_u, other_g, other_u, got_g, got_u

    def finish(keep_g, keep_u, other_g, other_u, got_g, got_u):
        gate = last_step(lambda j: keep_g[j] + other_g[j].astype(F32), got_g, "wid", low_steps)
        up = last_step(lambda j: keep_u[j] + other_u[j].astype(F32), got_u, "wid", high_steps)
        hidden = (jax.nn.silu(gate) * up).astype(BF16)
        hidden = spread(hidden, "wid", W)
        theirs = swap(hidden)
        return down(y_orders, ad, hidden, theirs, down_weight)

    outs = []
    state = start(0)
    for c in range(CHUNKS):
        later = start(c + 1) if c + 1 < CHUNKS else None
        held_a, away_a, held_b, away_b = finish(*state)
        if later is not None:
            held_a, got_g, got_u = lax.optimization_barrier((held_a, later[4], later[5]))
            state = later[:4] + (got_g, got_u)
        got_a = lax.ppermute(away_a, "y", low_steps[0])
        got_b = lax.ppermute(away_b, "y", high_steps[0])
        low = last_step(lambda j: held_a[j], got_a, "y", low_steps)
        high = last_step(lambda j: held_b[j], got_b, "y", high_steps)
        partial = jnp.concatenate([low.astype(BF16), high.astype(BF16)], axis=-1)
        partial = jnp.sum(send(partial, "z").astype(F32), axis=0).astype(BF16)
        outs.append(partial)
    out = jnp.concatenate(outs, axis=0)
    return out.reshape(total_rows // n_hid, batches, -1)


def rows_x(blocks):
    me = lax.axis_index("wid")
    full = lax.dynamic_update_index_in_dim(
        jnp.zeros_like(blocks), lax.dynamic_index_in_dim(blocks, me, 0, keepdims=False), me, 0
    )
    for k in (2, 1, 3):
        away = lax.dynamic_index_in_dim(blocks, (me + k) % W, 0, keepdims=False)
        value = lax.ppermute(away, "wid", [(i, (i + k) % W) for i in range(W)])
        full = lax.dynamic_update_index_in_dim(full, value, (me + W - k) % W, 0)
    return full


def solution(mesh):
    grid = Mesh(mesh.devices.reshape(Y, Z, W, 2), ("y", "z", "wid", "ad"))
    hid = ("y", "z")
    in_specs = (
        P(None, None, ("wid", "ad")),
        P(),
        P(("wid", "ad"), None, hid),
        P(hid, ("wid", "ad")),
        P(("y", "z", "wid"), "ad", None, None),
        P(("y", "z", "wid"), "ad", None, None),
    )
    return jax.shard_map(
        layer, mesh=grid, in_specs=in_specs, out_specs=P(hid, None, ("wid", "ad")), check_vma=False
    )
```

```python
import jax
import jax.numpy as jnp
from jax import lax
from jax.experimental import pallas as pl
from jax.experimental.pallas import tpu as pltpu
from jax.sharding import Mesh, PartitionSpec as P


CHUNKS = 2
Y, Z, W = 4, 8, 4
F32 = jnp.float32
BF16 = jnp.bfloat16
PAIRS = [(i, i ^ 1) for i in range(4)]
ACROSS = [(i, 3 - i) for i in range(4)]


def swap(value):
    return lax.ppermute(value, "ad", [(0, 1), (1, 0)])


def by_core(ad, mine, theirs):
    return jnp.where(ad == 0, mine, theirs), jnp.where(ad == 0, theirs, mine)


def send(blocks, axis):
    return lax.all_to_all(blocks, axis, split_axis=0, concat_axis=0, tiled=True)


def spread(value, axis, n):
    return send(jnp.broadcast_to(value[None], (n,) + value.shape), axis)


def ring_orders(me):
    side, far = me ^ 1, 3 - me
    return jnp.stack([me, far, side, 3 - side]), jnp.stack([me, side, far, far ^ 1])


def split_owners(expand, n, units):
    def body(x, o):
        for h in range(n):
            o[h] = x[:, h * units:(h + 1) * units]

    rank = expand.shape[0]
    return pl.pallas_call(
        body,
        out_shape=jax.ShapeDtypeStruct((n, rank, units), expand.dtype),
        cost_estimate=pl.CostEstimate(flops=0, bytes_accessed=4 * expand.size, transcendentals=0),
        name="split_owners",
    )(expand)


def order_rows(activations):
    total, batches, width = activations.shape
    count = total // (Y * Z * CHUNKS)
    rows = Y * count * batches

    def body(x, o):
        o[...] = x[...].reshape(rows, width)

    return pl.pallas_call(
        body,
        grid=(CHUNKS, Z),
        in_specs=[pl.BlockSpec((Y, None, count, batches, width), lambda c, z: (0, z, c, 0, 0))],
        out_specs=pl.BlockSpec((rows, width), lambda c, z: (c * Z + z, 0)),
        out_shape=jax.ShapeDtypeStruct((total * batches, width), activations.dtype),
        cost_estimate=pl.CostEstimate(flops=0, bytes_accessed=4 * activations.size, transcendentals=0),
        name="order_rows",
    )(activations.reshape(Y, Z, CHUNKS * count, batches, width))


def adapter_terms(inner, expand):
    n, slots, rank = inner.shape
    units = expand.shape[2]
    per = slots // Z
    group = 8

    def body(a, b, o):
        for k in range(0, group, 2):
            two = [
                jnp.dot(a[k + i], b[k + i], preferred_element_type=F32).reshape(Z, per, units) for i in range(2)
            ]
            o[:, k * per:(k + 2) * per, :] = jnp.concatenate(two, axis=1).astype(BF16)

    return pl.pallas_call(
        body,
        grid=(n // group,),
        in_specs=[
            pl.BlockSpec((group, slots, rank), lambda i: (i, 0, 0)),
            pl.BlockSpec((group, rank, units), lambda i: (i, 0, 0)),
        ],
        out_specs=pl.BlockSpec((Z, group * per, units), lambda i: (0, i, 0)),
        out_shape=jax.ShapeDtypeStruct((Z, n * per, units), BF16),
        compiler_params=pltpu.CompilerParams(vmem_limit_bytes=28 * 2**20),
        cost_estimate=pl.CostEstimate(
            flops=2 * n * slots * rank * units, bytes_accessed=4 * expand.size, transcendentals=0
        ),
        name="adapter_terms",
    )(inner, expand)


def gate_up_base(places, ad, acts, weights, chunk):
    _, units, width = weights.shape
    piece = acts.shape[0] // (CHUNKS * 2 * W)

    def body(s, xa, xk, w, ag, au, kg, ku):
        x = jnp.concatenate([xa[...], xk[...]], axis=0)
        for p, (away, keep) in enumerate(((ag, kg), (au, ku))):
            value = lax.dot_general(x, w[p], (((1,), (1,)), ((), ())), preferred_element_type=F32)
            away[...] = value[:piece]
            keep[...] = value[piece:]

    def rows_of(away):
        return lambda i, s: (chunk * 2 * W + (1 - s[0] if away else s[0]) * W + i, 0)

    def place_at(p):
        return lambda i, s: (s[1 + W * p + i], 0, 0)

    block = (None, piece, units)
    return pl.pallas_call(
        body,
        grid_spec=pltpu.PrefetchScalarGridSpec(
            num_scalar_prefetch=1,
            grid=(W,),
            in_specs=[
                pl.BlockSpec((piece, width), rows_of(True)),
                pl.BlockSpec((piece, width), rows_of(False)),
                pl.BlockSpec((2, units, width), lambda i, s: (0, 0, 0)),
            ],
            out_specs=[pl.BlockSpec(block, place_at(p)) for p in (0, 1, 0, 1)],
        ),
        out_shape=[jax.ShapeDtypeStruct((W, piece, units), F32)] * 4,
        cost_estimate=pl.CostEstimate(
            flops=8 * W * piece * units * width, bytes_accessed=16 * 2**20, transcendentals=0
        ),
        name="gate_up_base",
    )(jnp.concatenate([ad[None], places]).astype(jnp.int32), acts, acts, weights)


def add_terms(places, ad, base, codes, terms, chunk):
    _, piece, units = base[0].shape
    count = terms.shape[1]

    def body(s, ca, ck, ta, tk, bag, bau, bkg, bku, ag, au, kg, ku):
        wide = lax.broadcasted_iota(jnp.int32, (piece, count), 1)
        for c, t, ins, outs in ((ca, ta, (bag, bau), (ag, au)), (ck, tk, (bkg, bku), (kg, ku))):
            place = (c[...] == wide).astype(BF16)
            extra = jnp.dot(place, t[...], preferred_element_type=F32).astype(BF16).astype(F32)
            for p in range(2):
                outs[p][...] = (ins[p][...] + jnp.where(s[0] == p, extra, 0.0)).astype(outs[p].dtype)

    def z_of(away, i, s):
        return (1 - s[0] if away else s[0]) * W + i

    def rows_of(away):
        return lambda i, s: (chunk * 2 * W + z_of(away, i, s), 0)

    def terms_of(away):
        return lambda i, s: (z_of(away, i, s), 0, 0)

    def place_at(p):
        return lambda i, s: (s[1 + W * p + i], 0, 0)

    places_of = [pl.BlockSpec((None, piece, units), place_at(p)) for p in (0, 1, 0, 1)]
    return pl.pallas_call(
        body,
        grid_spec=pltpu.PrefetchScalarGridSpec(
            num_scalar_prefetch=1,
            grid=(W,),
            in_specs=[
                pl.BlockSpec((piece, 1), rows_of(True)),
                pl.BlockSpec((piece, 1), rows_of(False)),
                pl.BlockSpec((None, count, units), terms_of(True)),
                pl.BlockSpec((None, count, units), terms_of(False)),
            ] + places_of,
            out_specs=places_of,
        ),
        out_shape=[jax.ShapeDtypeStruct((W, piece, units), d) for d in (BF16, BF16, F32, F32)],
        compiler_params=pltpu.CompilerParams(vmem_limit_bytes=28 * 2**20),
        cost_estimate=pl.CostEstimate(
            flops=4 * W * piece * units * count, bytes_accessed=14 * 2**20, transcendentals=0
        ),
        name="add_terms",
    )(jnp.concatenate([ad[None], places]).astype(jnp.int32), codes, codes, terms, terms, *base)


def down(orders, ad, mine, theirs, weight):
    _, piece, units = mine.shape
    width = weight.shape[1]
    part, cols = piece // Y, width // 2

    def body(s, m, t, w, held_a, away_a, held_b, away_b, full):
        x = jnp.where(pl.program_id(0) == 0, m[...], t[...]).reshape(W * piece, units)
        full[...] = jnp.dot(x, w[...], preferred_element_type=F32).reshape(W, piece, width)
        for f, (held, away) in enumerate(((held_a, away_a), (held_b, away_b))):
            for j in range(4):
                at = pl.multiple_of(s[1 + 4 * f + j] * part, 8)
                for i in range(W):
                    value = full[i, pl.ds(at, part), f * cols:(f + 1) * cols]
                    if j < 2:
                        held[j, i] = value
                    else:
                        away[j - 2, i] = value.astype(BF16)

    spec = pl.BlockSpec((2, W, part, cols), lambda e, s: (0, s[0] ^ e, 0, 0))
    whole = pl.BlockSpec((W, piece, units), lambda e, s: (0, 0, 0))
    return pl.pallas_call(
        body,
        grid_spec=pltpu.PrefetchScalarGridSpec(
            num_scalar_prefetch=1,
            grid=(2,),
            in_specs=[whole, whole, pl.BlockSpec((units, width), lambda e, s: (0, 0))],
            out_specs=[spec] * 4,
            scratch_shapes=[pltpu.VMEM((W, piece, width), F32)],
        ),
        out_shape=[jax.ShapeDtypeStruct((2, Z, part, cols), d) for d in (F32, BF16, F32, BF16)],
        compiler_params=pltpu.CompilerParams(vmem_limit_bytes=28 * 2**20),
        cost_estimate=pl.CostEstimate(
            flops=4 * W * piece * units * width, bytes_accessed=12 * 2**20, transcendentals=0
        ),
        name="down",
    )(jnp.concatenate([ad[None], orders]).astype(jnp.int32), mine, theirs, weight)


def first_step(held, others, axis, steps):
    away = (held[2:] + others[2:].astype(F32)).astype(BF16)
    return lax.ppermute(away, axis, steps[0])


def last_step(held, got, axis, steps):
    later = (held(1) + got[1].astype(F32)).astype(BF16)
    return held(0) + got[0].astype(F32) + lax.ppermute(later, axis, steps[1]).astype(F32)


def layer(activations, row_adapter_index, gate_up_weight, down_weight, shrink, expand):
    hid = lax.axis_index(("y", "z"))
    wid = lax.axis_index("wid")
    ad = lax.axis_index("ad")
    n_hid = Y * Z
    total_rows, batches, width = activations.shape
    rows = total_rows * batches
    block = rows // n_hid
    part = block // CHUNKS
    units = down_weight.shape[0]
    rank = shrink.shape[2]
    slots = 2 * n_hid

    by_owner = split_owners(expand[0, 0], n_hid, units)
    by_owner, activations = lax.optimization_barrier((by_owner, activations))
    expand_all = send(by_owner, ("y", "z"))

    acts = order_rows(activations)

    def to_chunks(flat):
        return flat.reshape(Y, Z, CHUNKS, part).transpose(2, 1, 0, 3)

    ids = row_adapter_index.reshape(n_hid, block)
    same = ids[:, :, None] == ids[:, None, :]
    earlier = jnp.arange(block)[None, :] < jnp.arange(block)[:, None]
    place = jnp.sum((same & earlier[None]).astype(jnp.int32), axis=2)
    member = jnp.arange(n_hid, dtype=jnp.int32)[:, None]
    near = 2 * (member // Z) + place
    slot = 2 * Y * (member % Z) + near
    owner, cls = ids // W, ids % W
    send_code = jnp.where(owner == hid, cls * slots + slot, -1)
    recv_code = jnp.where(cls == wid, 2 * Y * owner + near, -1)
    send_code = to_chunks(send_code).reshape(rows)
    recv_code = to_chunks(recv_code).reshape(rows, 1)

    weights = gate_up_weight.transpose(1, 2, 0)
    x_orders = ring_orders(wid)
    x_places = jnp.concatenate([
        jnp.sum(jnp.where(order[:, None] == jnp.arange(W)[None], jnp.arange(W)[:, None], 0), axis=0)
        for order in x_orders
    ])
    y_orders = jnp.concatenate(ring_orders(lax.axis_index("y")))
    bases = [gate_up_base(x_places, ad, acts, weights, c) for c in range(CHUNKS)]

    pick = (jnp.arange(W * slots, dtype=jnp.int32)[:, None] == send_code[None, :]).astype(BF16)
    picked = jnp.dot(pick, acts, preferred_element_type=F32).astype(BF16)
    mine = rows_x(picked.reshape(W, slots, width))
    theirs = swap(mine)
    first, second = by_core(ad, mine, theirs)
    shrink_blocks = shrink[0, 0].reshape(rank, W, 2, width)
    inner = jnp.einsum("xsf,jxf->sj", first, shrink_blocks[:, :, 0], preferred_element_type=F32)
    inner = inner + jnp.einsum("xsf,jxf->sj", second, shrink_blocks[:, :, 1], preferred_element_type=F32)
    inner, expand_all, bases[1:] = lax.optimization_barrier((inner.astype(BF16), expand_all, bases[1:]))
    inner_all = spread(inner, ("y", "z"), n_hid)
    terms = adapter_terms(inner_all, expand_all)

    low_steps, high_steps = (PAIRS, ACROSS), (ACROSS, PAIRS)

    def start(c):
        away_g, away_u, keep_g, keep_u = add_terms(x_places, ad, bases[c], recv_code, terms, c)
        other_g, other_u = swap(away_g), swap(away_u)
        got_g = first_step(keep_g, other_g, "wid", low_steps)
        got_u = first_step(keep_u, other_u, "wid", high_steps)
        return keep_g, keep_u, other_g, other_u, got_g, got_u

    def finish(keep_g, keep_u, other_g, other_u, got_g, got_u):
        gate = last_step(lambda j: keep_g[j] + other_g[j].astype(F32), got_g, "wid", low_steps)
        up = last_step(lambda j: keep_u[j] + other_u[j].astype(F32), got_u, "wid", high_steps)
        hidden = (jax.nn.silu(gate) * up).astype(BF16)
        hidden = spread(hidden, "wid", W)
        theirs = swap(hidden)
        return down(y_orders, ad, hidden, theirs, down_weight)

    outs = []
    state = start(0)
    for c in range(CHUNKS):
        later = start(c + 1) if c + 1 < CHUNKS else None
        held_a, away_a, held_b, away_b = finish(*state)
        if later is not None:
            held_a, got_g, got_u = lax.optimization_barrier((held_a, later[4], later[5]))
            state = later[:4] + (got_g, got_u)
        got_a = lax.ppermute(away_a, "y", low_steps[0])
        got_b = lax.ppermute(away_b, "y", high_steps[0])
        low = last_step(lambda j: held_a[j], got_a, "y", low_steps)
        high = last_step(lambda j: held_b[j], got_b, "y", high_steps)
        partial = jnp.concatenate([low.astype(BF16), high.astype(BF16)], axis=-1)
        partial = jnp.sum(send(partial, "z").astype(F32), axis=0).astype(BF16)
        outs.append(partial)
    out = jnp.concatenate(outs, axis=0)
    return out.reshape(total_rows // n_hid, batches, -1)


def rows_x(blocks):
    me = lax.axis_index("wid")
    full = lax.dynamic_update_index_in_dim(
        jnp.zeros_like(blocks), lax.dynamic_index_in_dim(blocks, me, 0, keepdims=False), me, 0
    )
    for k in (2, 1, 3):
        away = lax.dynamic_index_in_dim(blocks, (me + k) % W, 0, keepdims=False)
        value = lax.ppermute(away, "wid", [(i, (i + k) % W) for i in range(W)])
        full = lax.dynamic_update_index_in_dim(full, value, (me + W - k) % W, 0)
    return full


def solution(mesh):
    grid = Mesh(mesh.devices.reshape(Y, Z, W, 2), ("y", "z", "wid", "ad"))
    hid = ("y", "z")
    in_specs = (
        P(None, None, ("wid", "ad")),
        P(),
        P(("wid", "ad"), None, hid),
        P(hid, ("wid", "ad")),
        P(("y", "z", "wid"), "ad", None, None),
        P(("y", "z", "wid"), "ad", None, None),
    )
    return jax.shard_map(
        layer, mesh=grid, in_specs=in_specs, out_specs=P(hid, None, ("wid", "ad")), check_vma=False
    )
```
